32 devices in a mesh: row: 8 (over z, y), col: 4 (over x, core).
Axes of the slice: x: 2, y: 2, z: 4, core: 2. Of those that a mesh axis runs over, the one named last changes fastest.
Arguments:
- p_values: bfloat16 [128, 16, 128, 128], P('row', 'col'), may hold values from -0.5 to 0.5
- p_cols: int32 [128, 16], P('row', 'col'), may hold values from -1 to 127, as said below
- s_values: bfloat16 [128, 16, 128, 128], P('row', 'col'), may hold values from -1.796875 to 1.796875
- s_cols: int32 [128, 16], P('row', 'col'), may hold values from -1 to 127, as said below
- c_cols: int32 [128, 32], P('row', 'col'), may hold values from -1 to 127, as said below
Outputs:
- product: float32 [128, 32, 128, 128], P('row', 'col')
The draws below stay inside these ranges and needn't reach their ends.
Inputs may be any that keep to these rules, and one draw needn't show every extreme that they name: `p_cols`: each block row r of P holds distinct block columns c with (c - r) mod 128 in [-8, 8] taken cyclically; other slots are -1. `s_cols`: in block row q of S, slots g * 4 to (g + 1) * 4 - 1 hold distinct block columns c with c mod 4 = g and (c - q) mod 128 in [-8, 8] taken cyclically; other slots are -1. `c_cols`: in block row r, slots g * 8 to (g + 1) * 8 - 1 hold distinct block columns c with c mod 4 = g and (c - r) mod 128 in [-16, 16] taken cyclically; other slots are -1.
All inputs are finite; a program needn't handle non-finite values.
Results may differ from the reference program's by a relative error of at most 0.0003.
Values may be sent and summed in bfloat16 or wider, within the bound.
No kernel may reach another device: no remote copies, remote signals or barrier semaphores. Data moves between devices by JAX's collectives and lax.ppermute only.
A program may use at most 192 MiB of HBM per device.

```python
import jax
import jax.numpy as jnp
from jax import lax

B = 128
K = 16
KC = 32
HALF = 8
NB = 128
GROUPS = 4


def band_pick(key, span, slots_per, group_count):
    width = 2 * span + 1
    offsets = jnp.arange(width, dtype=jnp.int32) - span
    rows_index = jnp.arange(NB, dtype=jnp.int32)
    columns = (rows_index[:, None] + offsets[None, :]) % NB
    residue = columns % group_count
    taken = min(slots_per, width)
    pieces = []
    for group in range(group_count):
        gkey = jax.random.fold_in(key, group)
        valid = residue == group
        score = jax.random.randint(gkey, (NB, width), 0, 1 << 20) * width + jnp.arange(width, dtype=jnp.int32)[None, :]
        score = score + jnp.where(valid, 0, 1 << 30)
        order = jnp.argsort(score, axis=1, stable=True)[:, :taken]
        chosen = jnp.take_along_axis(columns, order, axis=1)
        chosen_ok = jnp.take_along_axis(valid, order, axis=1)
        keep = jax.random.randint(jax.random.fold_in(gkey, 7), (NB, taken), 0, 4) > 0
        picked = jnp.where(chosen_ok & keep, chosen, -1)
        if taken < slots_per:
            picked = jnp.concatenate([picked, -jnp.ones((NB, slots_per - taken), jnp.int32)], axis=1)
        pieces.append(picked)
    return jnp.concatenate(pieces, axis=1).astype(jnp.int32)


def draw_p_cols(key, part):
    return band_pick(jax.random.fold_in(key, 11), HALF, K, 1)


def draw_s_cols(key, part):
    return band_pick(jax.random.fold_in(key, 23), HALF, K // GROUPS, GROUPS)


def draw_c_cols(key, part):
    return band_pick(jax.random.fold_in(key, 37), 2 * HALF, KC // GROUPS, GROUPS)


def block_levels(rng, extent, shards, low, largest):
    level = 1.0
    for axis_at, parts in shards:
        draws = jax.random.uniform(jax.random.fold_in(jax.random.fold_in(rng, 6), axis_at), (parts,), jnp.float32, low / len(shards), largest / len(shards))
        level = level * jnp.repeat(jnp.exp(draws), extent[axis_at] // parts).reshape((-1,) + (1,) * (len(extent) - 1 - axis_at))
    return level


def noise(rng, extent, scale, limit, cuts=(), kind=jnp.bfloat16):
    values = jax.random.normal(rng, extent, jnp.float32) * scale
    if len(cuts) > 0:
        values = block_levels(rng, extent, cuts, -0.22, 0.18) * values
    return jnp.clip(values, min=-limit, max=limit).astype(kind)


def setup_inputs(seed: int = 0) -> dict:
    arg_keys = jax.random.split(jax.random.key(seed), 6)
    p_values = noise(arg_keys[0], (NB, K, B, B), B ** -0.5, 0.5, ((0, 8), (1, 4)))
    p_cols = draw_p_cols(jax.random.fold_in(arg_keys[5], 71), 0)
    s_values = noise(arg_keys[2], (NB, K, B, B), 0.3, 1.796875, ((0, 8), (1, 4)))
    s_cols = draw_s_cols(jax.random.fold_in(arg_keys[5], 71), 0)
    c_cols = draw_c_cols(jax.random.fold_in(arg_keys[5], 71), 0)
    return dict(p_values=p_values, p_cols=p_cols, s_values=s_values, s_cols=s_cols, c_cols=c_cols)


def reference(p_values, p_cols, s_values, s_cols, c_cols):
    def one_row(carry, items):
        row_vals, row_cols, kept_cols = items
        live = row_cols >= 0
        index = jnp.where(live, row_cols, 0).astype(jnp.int32)
        s_rows = s_values[index]
        s_row_cols = s_cols[index]
        pairs = jnp.einsum("kab,klbc->klac", row_vals.astype(jnp.float32), s_rows.astype(jnp.float32),
                           precision=lax.Precision.HIGHEST)
        match = ((s_row_cols[:, :, None] == kept_cols[None, None, :])
                 & (s_row_cols[:, :, None] >= 0) & live[:, None, None]).astype(jnp.float32)
        result = jnp.einsum("klm,klac->mac", match, pairs, precision=lax.Precision.HIGHEST)
        return carry, result

    unused, product = lax.scan(one_row, jnp.float32(0.0), (p_values, p_cols, c_cols))
    return product
```

```python
import functools

import jax
import jax.numpy as jnp
from jax import lax
from jax.experimental import pallas as pl
from jax.experimental.pallas import tpu as pltpu
from jax.sharding import PartitionSpec as P


def row_chunks(block_rows):
    edges, low = [], block_rows // 2
    while low > 0:
        low = low // 2
        edges.append(low)
    return edges


def both_ends(block, low, previous, block_rows):
    if previous == block_rows // 2:
        return block[low : block_rows - low]
    return jnp.concatenate(
        [block[low:previous], block[block_rows - previous : block_rows - low]], axis=0
    )


def gathered(block, own, axis):
    count = lax.axis_size(axis)
    if count & (count - 1):
        moved = [
            lax.ppermute(block, axis, [(i, (i + t) % count) for i in range(count)])
            for t in range(1, count)
        ]
        return [own] + moved
    held, sent, step = [own], [block], count // 2
    while step:
        swap = [(i, i ^ step) for i in range(count)]
        moved = [lax.ppermute(piece, axis, swap) for piece in sent]
        held, sent, step = held + moved, sent + moved, step // 2
    return held


def product_rows(place_ref, *refs, pieces, spans, rows, slots, kept, zero_at, aliased):
    p_refs, s_refs = refs[:pieces], refs[pieces : pieces + len(spans)]
    out_ref, window, sem = refs[pieces + len(spans) + aliased :]
    step = pl.program_id(0)
    copies = [
        pltpu.make_async_copy(ref, window.at[pl.ds(at, size)], sem.at[n])
        for n, (ref, (at, size)) in enumerate(zip(s_refs, spans))
    ]

    @pl.when(step == 0)
    def _():
        for copy in copies:
            copy.start()
        window[zero_at] = jnp.zeros(window.shape[1:], window.dtype)
        for copy in copies:
            copy.wait()

    left = jnp.concatenate(
        [ref[0, slot] for ref in p_refs for slot in range(ref.shape[1])], axis=1
    )
    wide = 2 if kept % 2 == 0 else 1
    for m in range(0, kept, wide):
        right = jnp.concatenate(
            [
                jnp.concatenate(
                    [window[place_ref[step, k * kept + m + n]] for n in range(wide)], axis=1
                )
                for k in range(slots)
            ],
            axis=0,
        )
        result = jnp.dot(left, right, preferred_element_type=jnp.float32)
        order = result.shape[1] // wide
        for n in range(wide):
            out_ref[0, m + n] = result[:, n * order : (n + 1) * order]


def shards(p_values, p_cols, s_values, s_cols, c_cols):
    block_rows, own_slots, order, _ = p_values.shape
    s_slots, kept = s_values.shape[1], c_cols.shape[1]
    reach = block_rows // 2
    row_count, col_count = lax.axis_size("row"), lax.axis_size("col")
    total_rows = block_rows * row_count
    first_row = lax.axis_index("row") * block_rows - reach
    forward = [(i, (i + 1) % row_count) for i in range(row_count)]
    backward = [(target, source) for source, target in forward]
    edges = row_chunks(block_rows)
    befores = [reach] + edges[:-1]

    p_parts, low_parts, high_parts = [], [], []
    for low, previous in zip(edges, befores):
        chunk = both_ends(p_values, low, previous, block_rows)
        p_parts.append(chunk)
        low_parts.append(
            lax.ppermute(
                s_values[block_rows + low - reach : block_rows + previous - reach], "row", forward
            )
        )
        high_parts.append(
            lax.ppermute(s_values[reach - previous : reach - low], "row", backward)
        )
    p_gathered = [gathered(chunk, p_values, "col") for chunk in p_parts]

    all_p_cols = jnp.concatenate(gathered(p_cols, p_cols, "col"), axis=1)
    near_cols = jnp.concatenate(
        [
            lax.ppermute(s_cols[block_rows - reach :], "row", forward),
            s_cols,
            lax.ppermute(s_cols[:reach], "row", backward),
        ],
        axis=0,
    )
    window_rows = near_cols.shape[0]
    slots = all_p_cols.shape[1]
    zero_at = window_rows * s_slots
    local = jnp.where(all_p_cols >= 0, (all_p_cols - first_row) % total_rows, -1)
    flat_cols = near_cols.reshape(-1)
    at = lax.broadcasted_iota(jnp.int32, (1, 1, 1, zero_at), 3)
    hit = (
        (local[:, :, None, None] == at // s_slots)
        & (flat_cols[None, None, None, :] == c_cols[:, None, :, None])
        & (flat_cols[None, None, None, :] >= 0)
    )
    place = jnp.min(jnp.where(hit, at, zero_at), axis=3).reshape(block_rows, slots * kept)

    flat = lambda block: block.reshape((-1, order, order))
    product = None
    pairs = [(flat(s_values), (reach * s_slots, block_rows * s_slots))]
    for n, (low, previous) in enumerate(zip(edges, befores)):
        pairs = pairs + [
            (flat(low_parts[n]), (low * s_slots, (previous - low) * s_slots)),
            (
                flat(high_parts[n]),
                ((block_rows + 2 * reach - previous) * s_slots, (previous - low) * s_slots),
            ),
        ]
        half = previous - low
        count = 2 * half
        row_of = lambda i, low=low, half=half, previous=previous: jnp.where(
            i < half, low + i, block_rows - previous + i - half
        )
        p_specs = [
            pl.BlockSpec(
                (1, own_slots, order, order),
                (lambda i, place, row_of=row_of: (row_of(i), 0, 0, 0))
                if t == 0
                else (lambda i, place: (i, 0, 0, 0)),
            )
            for t in range(col_count)
        ]
        aliased = int(product is not None)
        any_spec = pl.BlockSpec(memory_space=pl.ANY)
        call = pl.pallas_call(
            functools.partial(
                product_rows,
                pieces=col_count,
                spans=tuple(span for _, span in pairs),
                rows=count,
                slots=slots,
                kept=kept,
                zero_at=zero_at,
                aliased=aliased,
            ),
            out_shape=jax.ShapeDtypeStruct((block_rows, kept, order, order), jnp.float32),
            grid_spec=pltpu.PrefetchScalarGridSpec(
                num_scalar_prefetch=1,
                grid=(count,),
                in_specs=p_specs + [any_spec] * (len(pairs) + aliased),
                out_specs=pl.BlockSpec(
                    (1, kept, order, order), lambda i, place, row_of=row_of: (row_of(i), 0, 0, 0)
                ),
                scratch_shapes=[
                    pltpu.VMEM((zero_at + 1, order, order), s_values.dtype),
                    pltpu.SemaphoreType.DMA((len(pairs),)),
                ],
            ),
            input_output_aliases={1 + col_count + len(pairs): 0} if aliased else {},
            name=f"rows_{n}",
        )
        product = call(
            both_ends(place, low, previous, block_rows),
            *p_gathered[n],
            *[piece for piece, _ in pairs],
            *([product] if aliased else []),
        )
    return product


def solution(mesh):
    return jax.shard_map(
        shards,
        mesh=mesh,
        in_specs=(
            P("row", "col", None, None),
            P("row", "col"),
            P("row", "col", None, None),
            P("row", "col"),
            P("row", "col"),
        ),
        out_specs=P("row", "col", None, None),
        check_vma=False,
    )
```

```python
import functools

import jax
import jax.numpy as jnp
from jax import lax
from jax.experimental import pallas as pl
from jax.experimental.pallas import tpu as pltpu
from jax.sharding import PartitionSpec as P

VMEM_GRANT = 16 << 20
ANY = pl.BlockSpec(memory_space=pl.ANY)
SMEM = pl.BlockSpec(memory_space=pltpu.SMEM)
VMEM = pl.BlockSpec(memory_space=pltpu.VMEM)


def in_vmem(array):
    return pltpu.with_memory_space_constraint(array, pltpu.VMEM)


def in_hbm(array):
    return pltpu.with_memory_space_constraint(array, pltpu.HBM)


def row_chunks(block_rows):
    reach = block_rows // 2
    edges = [0, reach]
    for left in (reach // 2, reach // 4, 0):
        if block_rows - left > edges[-1]:
            edges.append(block_rows - left)
    return list(zip(edges[:-1], edges[1:]))


def local_start(part, block_rows, flip):
    start, stop = part
    return jnp.where(flip == 1, block_rows - stop, start)


def window_start(part, block_rows, flip):
    start, stop = part
    reach = block_rows // 2
    if start < reach:
        return jnp.where(flip == 1, reach + block_rows + start, reach - stop)
    return jnp.where(flip == 1, start - block_rows + reach, reach + 2 * block_rows - stop)


def cut(flips, p_values, s_values, cuts):
    block_rows = p_values.shape[0]
    sources = (p_values, s_values)

    def body(flips_ref, *refs):
        ins, outs, sems = refs[:2], refs[2:-1], refs[-1]
        copies = [
            pltpu.make_async_copy(
                ins[source].at[
                    pl.ds(local_start(part, block_rows, flips_ref[source]), out.shape[0])
                ],
                out,
                sems.at[n],
            )
            for n, ((source, part), out) in enumerate(zip(cuts, outs))
        ]
        for copy in copies:
            copy.start()
        for copy in copies:
            copy.wait()

    shapes = [
        jax.ShapeDtypeStruct((part[1] - part[0],) + sources[source].shape[1:], p_values.dtype)
        for source, part in cuts
    ]
    return list(
        pl.pallas_call(
            body,
            out_shape=shapes,
            in_specs=[SMEM, ANY, ANY],
            out_specs=[VMEM] * len(shapes),
            scratch_shapes=[pltpu.SemaphoreType.DMA((len(cuts),))],
            compiler_params=pltpu.CompilerParams(vmem_limit_bytes=VMEM_GRANT),
        )(flips, in_hbm(p_values), in_hbm(s_values))
    )


def find_places(first_ref, flip_ref, near_ref, own_ref, far_ref, kept_ref, *refs, total_rows):
    p_refs, place_ref = refs[:-1], refs[-1]
    kept, block_rows = kept_ref.shape
    s_slots, reach = own_ref.shape[0], block_rows // 2
    shape = place_ref.shape
    lane = lax.broadcasted_iota(jnp.int32, shape, 1)
    p_cols = jnp.full(shape, -1, jnp.int32)
    k = 0
    for ref in p_refs:
        cols = ref[...].T
        for slot in range(cols.shape[1]):
            p_cols = jnp.where(lane // kept == k, cols[:, slot : slot + 1], p_cols)
            k += 1
    wanted = jnp.full(shape, -2, jnp.int32)
    cols = kept_ref[...].T
    for m in range(kept):
        wanted = jnp.where(lane % kept == m, cols[:, m : m + 1], wanted)
    wanted = jnp.where(wanted < 0, -2, wanted)
    first_row = first_ref[0]
    local = p_cols - first_row
    local = jnp.where(local < 0, local + total_rows, local)
    local = jnp.where(local >= total_rows, local - total_rows, local)
    local = jnp.where(p_cols < 0, -1, local)
    flipped = flip_ref[0] == 1
    none = 2 * block_rows * s_slots
    place = jnp.full(shape, none, jnp.int32)
    for q in range(2 * block_rows):
        here = local == q
        for slot in range(s_slots):
            if q < reach:
                near, far = near_ref[slot, q + reach], far_ref[slot, q + reach]
                col = jnp.where(flipped, far, near)
            elif q < reach + block_rows:
                col = own_ref[slot, q - reach]
            else:
                row = q - reach - block_rows
                col = jnp.where(flipped, near_ref[slot, row], far_ref[slot, row])
            place = jnp.where(here & (wanted == col), q * s_slots + slot, place)
    place_ref[...] = place


def multiply(flip_ref, place_ref, *refs, pieces, chunk, block_rows, kept, news, first):
    p_refs = refs[: len(pieces)]
    new_refs = refs[len(pieces) : len(pieces) + len(news)]
    rest = refs[len(pieces) + len(news) + (0 if first else 2) :]
    out_ref, window, lefts, results, new_sem, p_sems, out_sems = rest
    flip = flip_ref[0]
    start = local_start(chunk, block_rows, flip)
    count = chunk[1] - chunk[0]
    slots, s_slots = lefts.shape[1], (window.shape[0] - 1) // (2 * block_rows)
    own_slots = slots // len(pieces)
    wide = max(w for w in (4, 2, 1) if kept % w == 0)
    order = window.shape[1]

    def fetch(i, n):
        return pltpu.make_async_copy(
            p_refs[n].at[start + i if pieces[n] else i],
            lefts.at[i, pl.ds(n * own_slots, own_slots)],
            p_sems.at[i],
        )

    def store(i, m):
        return pltpu.make_async_copy(
            results.at[i % 2, pl.ds(m, wide)],
            out_ref.at[start + i, pl.ds(m, wide)],
            out_sems.at[i % 2],
        )

    def stored(i):
        return pltpu.make_async_copy(
            results.at[i % 2], out_ref.at[start + i], out_sems.at[i % 2]
        )

    def fetch_row(i):
        for n in range(len(pieces)):
            fetch(i, n).start()

    copies = []
    for n, (ref, part) in enumerate(zip(new_refs, news)):
        at = block_rows // 2 if part is None else window_start(part, block_rows, flip)
        target = window.at[pl.ds(at * s_slots, ref.shape[0] * s_slots)]
        target = target.reshape(ref.shape)
        copies.append(pltpu.make_async_copy(ref, target, new_sem.at[n]))
    for copy in copies:
        copy.start()
    for i in range(min(2, count)):
        fetch_row(i)
    if first:
        window[window.shape[0] - 1] = jnp.zeros(window.shape[1:], window.dtype)
    for copy in copies:
        copy.wait()

    def one_row(i, carry):
        pltpu.make_async_copy(lefts.at[i], lefts.at[i], p_sems.at[i]).wait()

        @pl.when(i + 2 < count)
        def _():
            fetch_row(i + 2)

        @pl.when(i >= 2)
        def _():
            stored(i - 2).wait()

        left = jnp.concatenate([lefts[i, slot] for slot in range(slots)], axis=1)
        for m in range(0, kept, wide):
            right = jnp.concatenate(
                [
                    jnp.concatenate(
                        [
                            window[place_ref[start + i, k * kept + m + n]]
                            for n in range(wide)
                        ],
                        axis=1,
                    )
                    for k in range(slots)
                ],
                axis=0,
            )
            result = jnp.dot(left, right, preferred_element_type=jnp.float32)
            for n in range(wide):
                results[i % 2, m + n] = result[:, n * order : (n + 1) * order]
            store(i, m).start()
        return carry

    lax.fori_loop(0, count, one_row, 0)
    for i in range(max(0, count - 2), count):
        stored(i).wait()


def turn_pairs(count, step):
    return [(i, (i + step) % count) for i in range(count)]


def far_pieces(own):
    count = lax.axis_size("col")
    held = [own]
    if count & (count - 1):
        for step in range(1, count):
            held.append(lax.ppermute(own, "col", turn_pairs(count, step)))
        return held
    step = count // 2
    while step > 1:
        swap = [(i, i ^ step) for i in range(count)]
        held = held + [lax.ppermute(piece, "col", swap) for piece in held]
        step //= 2
    return held


def passed_pieces(pieces):
    count = lax.axis_size("col")
    if count == 1 or count & (count - 1):
        return []
    return [
        lax.ppermute(piece, "col", [(i, i ^ 1) for i in range(count)]) for piece in pieces
    ]


def steps(p_values, p_cols, s_values, s_cols, c_cols):
    block_rows, own_slots, order, _ = p_values.shape
    s_slots, kept = s_values.shape[1], c_cols.shape[1]
    reach = block_rows // 2
    row_count = lax.axis_size("row")
    first_row = lax.axis_index("row") * block_rows - reach
    if row_count % 2 == 0:
        first_pairs = [(i, (i + (1 if i % 2 else -1)) % row_count) for i in range(row_count)]
        second_pairs = [(i, i ^ 1) for i in range(row_count)]
        odd = (lax.axis_index("row") % 2).astype(jnp.int32)
        flips = jnp.stack([odd, odd])
    else:
        first_pairs, second_pairs = turn_pairs(row_count, 1), turn_pairs(row_count, -1)
        flips = jnp.arange(2, dtype=jnp.int32)
    chunks = row_chunks(block_rows)
    sides = [chunks[0]] + [(block_rows + reach - b, block_rows + reach - a) for a, b in chunks[1:]]

    parts = cut(flips, p_values, s_values, [(0, chunks[0]), (1, sides[0])])
    rest = [(0, chunk) for chunk in chunks[1:]] + [(1, side) for side in sides[1:]]
    rest = cut(flips, p_values, s_values, rest)
    own = [parts[0]] + rest[: len(sides) - 1]
    sent = [parts[1]] + rest[len(sides) - 1 :]

    far = [far_pieces(piece) for piece in own]
    halo = []
    for n, piece in enumerate(sent):
        halo.append(lax.ppermute(piece, "row", second_pairs if n else first_pairs))
    core = passed_pieces([p_values])
    far_cols = far_pieces(p_cols.T)
    passed_cols = passed_pieces(far_cols)
    first_cols = lax.ppermute(s_cols.T, "row", first_pairs)
    second_cols = lax.ppermute(s_cols.T, "row", second_pairs)

    place = pl.pallas_call(
        functools.partial(find_places, total_rows=block_rows * row_count),
        out_shape=jax.ShapeDtypeStruct(
            (block_rows, len(far_cols + passed_cols) * own_slots * kept), jnp.int32
        ),
        in_specs=[SMEM] * 5 + [VMEM] * (1 + len(far_cols + passed_cols)),
        out_specs=VMEM,
        compiler_params=pltpu.CompilerParams(vmem_limit_bytes=VMEM_GRANT),
        name="places",
    )(first_row[None], flips, first_cols, s_cols.T, second_cols, c_cols.T, *far_cols, *passed_cols)

    product = None
    window_shape = (2 * block_rows * s_slots + 1, order, order)
    for n, chunk in enumerate(chunks):
        first = product is None
        count = chunk[1] - chunk[0]
        passed = passed_pieces(far[n][1:])
        held = [(piece, False) for piece in far[n]]
        held += [(piece, True) for piece in core] + [(piece, False) for piece in passed]
        if first:
            news, arrived = [None, sides[n]], [s_values, halo[n]]
        else:
            news, arrived = [sides[n]], [halo[n]]
        inputs = [flips, place] + [in_hbm(piece) for piece, _ in held]
        inputs += [in_hbm(piece) for piece in arrived]
        specs = [SMEM] * 2 + [ANY] * (len(inputs) - 2)
        aliases = {}
        if not first:
            aliases = {len(inputs): 1, len(inputs) + 1: 0}
            inputs += [in_vmem(window), product]
            specs += [VMEM, ANY]
        product, window = pl.pallas_call(
            functools.partial(
                multiply,
                pieces=tuple(whole for _, whole in held),
                chunk=chunk,
                block_rows=block_rows,
                kept=kept,
                news=tuple(news),
                first=first,
            ),
            out_shape=[
                jax.ShapeDtypeStruct((block_rows, kept, order, order), jnp.float32),
                pltpu.VMEM(window_shape, s_values.dtype),
            ],
            in_specs=specs,
            out_specs=[ANY, VMEM],
            scratch_shapes=[
                pltpu.VMEM((count, len(held) * own_slots, order, order), p_values.dtype),
                pltpu.VMEM((2, kept, order, order), jnp.float32),
                pltpu.SemaphoreType.DMA((len(news),)),
                pltpu.SemaphoreType.DMA((count,)),
                pltpu.SemaphoreType.DMA((2,)),
            ],
            input_output_aliases=aliases,
            compiler_params=pltpu.CompilerParams(vmem_limit_bytes=VMEM_GRANT),
        )(*inputs)
    return product


def solution(mesh):
    return jax.shard_map(
        steps,
        mesh=mesh,
        in_specs=(
            P("row", "col", None, None),
            P("row", "col"),
            P("row", "col", None, None),
            P("row", "col"),
            P("row", "col"),
        ),
        out_specs=P("row", "col", None, None),
        check_vma=False,
    )
```

```python
import functools

import jax
import jax.numpy as jnp
from jax import lax
from jax.experimental import pallas as pl
from jax.experimental.pallas import tpu as pltpu
from jax.sharding import PartitionSpec as P

VMEM_GRANT = 16 << 20
SECOND_EIGHTHS = (5, 3)
ANY = pl.BlockSpec(memory_space=pl.ANY)
SMEM = pl.BlockSpec(memory_space=pltpu.SMEM)
VMEM = pl.BlockSpec(memory_space=pltpu.VMEM)


def in_vmem(array):
    return pltpu.with_memory_space_constraint(array, pltpu.VMEM)


def in_hbm(array):
    return pltpu.with_memory_space_constraint(array, pltpu.HBM)


def row_chunks(block_rows):
    reach = block_rows // 2
    middle = reach // 2
    chunks = [(middle, reach), (0, middle)] if middle else [(0, reach)]
    start = reach
    for eighths in SECOND_EIGHTHS:
        stop = min(block_rows, start + max(1, eighths * reach // 8))
        if start < stop:
            chunks.append((start, stop))
            start = stop
    if start < block_rows:
        chunks.append((start, block_rows))
    return chunks


def halo_part(chunk, block_rows):
    start, stop = chunk
    reach = block_rows // 2
    if start < reach:
        return reach - stop, reach - start
    return block_rows + reach - stop, block_rows + reach - start


def local_start(part, block_rows, flip):
    start, stop = part
    return jnp.where(flip == 1, block_rows - stop, start)


def window_start(part, block_rows, flip):
    start, stop = part
    reach = block_rows // 2
    if start < reach:
        return jnp.where(flip == 1, reach + block_rows + start, reach - stop)
    return jnp.where(flip == 1, start - block_rows + reach, reach + 2 * block_rows - stop)


def cut(flips, p_values, s_values, cuts):
    block_rows = p_values.shape[0]
    sources = (p_values, s_values)

    def body(flips_ref, *refs):
        ins, outs, sems = refs[:2], refs[2:-1], refs[-1]
        copies = [
            pltpu.make_async_copy(
                ins[source].at[
                    pl.ds(local_start(part, block_rows, flips_ref[source]), out.shape[0])
                ],
                out,
                sems.at[n],
            )
            for n, ((source, part), out) in enumerate(zip(cuts, outs))
        ]
        for copy in copies:
            copy.start()
        for copy in copies:
            copy.wait()

    shapes = [
        jax.ShapeDtypeStruct((part[1] - part[0],) + sources[source].shape[1:], p_values.dtype)
        for source, part in cuts
    ]
    return list(
        pl.pallas_call(
            body,
            out_shape=shapes,
            in_specs=[SMEM, ANY, ANY],
            out_specs=[VMEM] * len(shapes),
            scratch_shapes=[pltpu.SemaphoreType.DMA((len(cuts),))],
            compiler_params=pltpu.CompilerParams(vmem_limit_bytes=VMEM_GRANT),
        )(flips, in_hbm(p_values), in_hbm(s_values))
    )


def find_places(first_ref, flip_ref, own_ref, near_ref, *refs, total_rows, both):
    far_ref = refs[0] if both else None
    kept_ref, *p_refs, place_ref = refs[1 if both else 0 :]
    kept, block_rows = kept_ref.shape
    s_slots, reach = own_ref.shape[0], block_rows // 2
    shape = place_ref.shape
    lane = lax.broadcasted_iota(jnp.int32, shape, 1)
    p_cols = jnp.full(shape, -1, jnp.int32)
    k = 0
    for ref in p_refs:
        cols = ref[...].T
        for slot in range(cols.shape[1]):
            p_cols = jnp.where(lane // kept == k, cols[:, slot : slot + 1], p_cols)
            k += 1
    wanted = jnp.full(shape, -2, jnp.int32)
    cols = kept_ref[...].T
    for m in range(kept):
        wanted = jnp.where(lane % kept == m, cols[:, m : m + 1], wanted)
    wanted = jnp.where(wanted < 0, -2, wanted)
    first_row = first_ref[0]
    local = p_cols - first_row
    local = jnp.where(local < 0, local + total_rows, local)
    local = jnp.where(local >= total_rows, local - total_rows, local)
    local = jnp.where(p_cols < 0, -1, local)
    flipped = flip_ref[0] == 1
    none = 2 * block_rows * s_slots
    place = jnp.full(shape, none, jnp.int32)
    for q in range(2 * block_rows):
        here = local == q
        for slot in range(s_slots):
            if reach <= q < reach + block_rows:
                col = own_ref[slot, q - reach]
            else:
                row = q + reach if q < reach else q - reach - block_rows
                far = far_ref[slot, row] if both else jnp.int32(-1)
                low_near = (q < reach) != flipped
                col = jnp.where(low_near, near_ref[slot, row], far)
            place = jnp.where(here & (wanted == col), q * s_slots + slot, place)
    place_ref[...] = place


def multiply(*refs, kinds, chunk, ahead, block_rows, kept, news, first):
    refs = list(refs)
    take = lambda count: [refs.pop(0) for _ in range(count)]
    flips_ref, place_ref = take(2)
    p_refs, new_refs = take(len(kinds)), take(len(news))
    take(0 if first else 2)
    ahead_refs = take(kinds.count("fetch") if ahead else 0)
    out_ref, window = take(2)
    next_ref = take(1)[0] if ahead else None
    lefts = take(1)[0] if first else None
    results, new_sem, p_sems, out_sems, next_sem = refs
    flip = flips_ref[0]
    start = local_start(chunk, block_rows, flip)
    count = chunk[1] - chunk[0]
    s_slots = (window.shape[0] - 1) // (2 * block_rows)
    own_slots = place_ref.shape[1] // (kept * len(kinds))
    wide = max(w for w in (4, 2, 1) if kept % w == 0)
    order = window.shape[1]
    slots = own_slots * len(kinds)
    fetched = [n for n, kind in enumerate(kinds) if kind == "fetch"]

    def fetch(i, n):
        return pltpu.make_async_copy(
            p_refs[n].at[i if n == 0 else start + i],
            lefts.at[i, pl.ds(fetched.index(n) * own_slots, own_slots)],
            p_sems.at[i],
        )

    def store(i, m):
        return pltpu.make_async_copy(
            results.at[i % 2, pl.ds(m, wide)],
            out_ref.at[start + i, pl.ds(m, wide)],
            out_sems.at[i % 2],
        )

    def stored(i):
        return pltpu.make_async_copy(
            results.at[i % 2], out_ref.at[start + i], out_sems.at[i % 2]
        )

    def left_blocks(i):
        for n, ref in enumerate(p_refs):
            for slot in range(own_slots):
                if kinds[n] != "fetch":
                    yield ref[i, slot]
                else:
                    source = lefts if first else p_refs[0]
                    yield source[i, fetched.index(n) * own_slots + slot]

    copies, moves = [], []
    for n, (ref, part) in enumerate(zip(new_refs, news)):
        at = block_rows // 2 if part is None else window_start(part, block_rows, flip)
        if first:
            target = window.at[pl.ds(at * s_slots, ref.shape[0] * s_slots)]
            target = target.reshape(ref.shape)
            copies.append(pltpu.make_async_copy(ref, target, new_sem.at[n]))
        else:
            moves.append((ref, at))
    for copy in copies:
        copy.start()
    if first:
        for i in range(count):
            for n in fetched:
                fetch(i, n).start()
        window[window.shape[0] - 1] = jnp.zeros(window.shape[1:], window.dtype)
    if ahead:
        next_start = local_start(ahead, block_rows, flip)
        next_count = ahead[1] - ahead[0]
        later = [
            pltpu.make_async_copy(
                ref.at[pl.ds(next_start if n else 0, next_count)],
                next_ref.at[:, pl.ds(n * own_slots, own_slots)],
                next_sem.at[n],
            )
            for n, ref in enumerate(ahead_refs)
        ]
        for copy in later:
            copy.start()
    for ref, at in moves:
        for row in range(ref.shape[0]):
            for slot in range(s_slots):
                window[(at + row) * s_slots + slot] = ref[row, slot]
    for copy in copies:
        copy.wait()

    def one_row(i, carry):
        if first:
            pltpu.make_async_copy(lefts.at[i], lefts.at[i], p_sems.at[i]).wait()

        @pl.when(i >= 2)
        def _():
            stored(i - 2).wait()

        left = jnp.concatenate(list(left_blocks(i)), axis=1)
        for m in range(0, kept, wide):
            right = jnp.concatenate(
                [
                    jnp.concatenate(
                        [
                            window[place_ref[start + i, k * kept + m + n]]
                            for n in range(wide)
                        ],
                        axis=1,
                    )
                    for k in range(slots)
                ],
                axis=0,
            )
            result = jnp.dot(left, right, preferred_element_type=jnp.float32)
            for n in range(wide):
                results[i % 2, m + n] = result[:, n * order : (n + 1) * order]
            store(i, m).start()
        return carry

    lax.fori_loop(0, count, one_row, 0)
    for i in range(max(0, count - 2), count):
        stored(i).wait()
    if ahead:
        for copy in later:
            copy.wait()


def turn_pairs(count, step):
    return [(i, (i + step) % count) for i in range(count)]


def far_pieces(own):
    count = lax.axis_size("col")
    held = [own]
    if count & (count - 1):
        for step in range(1, count):
            held.append(lax.ppermute(own, "col", turn_pairs(count, step)))
        return held
    step = count // 2
    while step > 1:
        swap = [(i, i ^ step) for i in range(count)]
        held = held + [lax.ppermute(piece, "col", swap) for piece in held]
        step //= 2
    return held


def passed_pieces(pieces):
    count = lax.axis_size("col")
    if count == 1 or count & (count - 1):
        return []
    return [
        lax.ppermute(piece, "col", [(i, i ^ 1) for i in range(count)]) for piece in pieces
    ]


def steps(p_values, p_cols, s_values, s_cols, c_cols):
    block_rows, own_slots, order, _ = p_values.shape
    s_slots, kept = s_values.shape[1], c_cols.shape[1]
    reach = block_rows // 2
    row_count = lax.axis_size("row")
    first_row = lax.axis_index("row") * block_rows - reach
    if row_count % 2 == 0:
        first_pairs = [(i, (i + (1 if i % 2 else -1)) % row_count) for i in range(row_count)]
        second_pairs = [(i, i ^ 1) for i in range(row_count)]
        odd = (lax.axis_index("row") % 2).astype(jnp.int32)
        flips = jnp.stack([odd, odd])
    else:
        first_pairs, second_pairs = turn_pairs(row_count, 1), turn_pairs(row_count, -1)
        flips = jnp.arange(2, dtype=jnp.int32)
    chunks = row_chunks(block_rows)
    sides = [halo_part(chunk, block_rows) for chunk in chunks]

    lead = next(n for n, chunk in enumerate(chunks) if chunk[0] >= reach)
    wanted = [(0, chunk) for chunk in chunks] + [(1, side) for side in sides]
    early = [0, len(chunks) + lead, len(chunks)]
    late = [n for n in range(len(wanted)) if n not in early]
    pieces = dict(zip(early, cut(flips, p_values, s_values, [wanted[n] for n in early])))
    pieces |= zip(late, cut(flips, p_values, s_values, [wanted[n] for n in late]))
    own = [pieces[n] for n in range(len(chunks))]
    sent = [pieces[len(chunks) + n] for n in range(len(chunks))]

    far = [far_pieces(piece) for piece in own]
    halo = []
    for n, piece in enumerate(sent):
        pairs = first_pairs if chunks[n][0] < reach else second_pairs
        halo.append(lax.ppermute(piece, "row", pairs))
    core = passed_pieces([p_values])
    far_cols = far_pieces(p_cols.T)
    passed_cols = passed_pieces(far_cols)
    first_cols = lax.ppermute(s_cols.T, "row", first_pairs)
    second_cols = lax.ppermute(s_cols.T, "row", second_pairs)

    col_pieces = far_cols + passed_cols

    def places(both):
        tables = [first_row[None], flips, s_cols.T, first_cols] + ([second_cols] if both else [])
        return pl.pallas_call(
            functools.partial(find_places, total_rows=block_rows * row_count, both=both),
            out_shape=jax.ShapeDtypeStruct(
                (block_rows, len(col_pieces) * own_slots * kept), jnp.int32
            ),
            in_specs=[SMEM] * len(tables) + [VMEM] * (1 + len(col_pieces)),
            out_specs=VMEM,
            compiler_params=pltpu.CompilerParams(vmem_limit_bytes=VMEM_GRANT),
        )(*tables, c_cols.T, *col_pieces)

    place_of = [places(False), places(True)]

    product = window = ready = None
    window_shape = (2 * block_rows * s_slots + 1, order, order)
    fetches = 1 + len(core)
    for n, chunk in enumerate(chunks):
        first = product is None
        count = chunk[1] - chunk[0]
        ahead = chunks[n + 1] if n + 1 < len(chunks) else None
        passed = passed_pieces(far[n][1:])
        kinds = ["fetch"] + ["here"] * len(far[n][1:]) + ["fetch"] * len(core)
        kinds += ["here"] * len(passed)
        fetch_from = [far[n][0]] + core
        here = far[n][1:] + passed
        inputs, specs = [flips, place_of[chunk[0] >= reach]], [SMEM] * 2
        for kind in kinds:
            if kind == "here":
                inputs.append(in_vmem(here.pop(0)))
            else:
                inputs.append(in_hbm(fetch_from.pop(0)) if first else ready)
            specs.append(ANY if first and kind == "fetch" else VMEM)
        aliases = {}
        if first:
            news = [None, sides[n]]
            inputs += [in_hbm(s_values), in_hbm(halo[n])]
            specs += [ANY] * 2
        else:
            news = [sides[n]]
            inputs.append(in_vmem(halo[n]))
            specs.append(VMEM)
            aliases = {len(inputs): 1, len(inputs) + 1: 0}
            inputs += [in_vmem(window), product]
            specs += [VMEM, ANY]
        outs = [
            jax.ShapeDtypeStruct((block_rows, kept, order, order), jnp.float32),
            pltpu.VMEM(window_shape, s_values.dtype),
        ]
        if ahead:
            inputs += [in_hbm(own[n + 1])] + [in_hbm(piece) for piece in core]
            specs += [ANY] * fetches
            shape = (ahead[1] - ahead[0], fetches * own_slots, order, order)
            outs.append(pltpu.VMEM(shape, p_values.dtype))
        scratch = [
            pltpu.VMEM((2, kept, order, order), jnp.float32),
            pltpu.SemaphoreType.DMA((2,)),
            pltpu.SemaphoreType.DMA((count,)),
            pltpu.SemaphoreType.DMA((2,)),
            pltpu.SemaphoreType.DMA((fetches,)),
        ]
        if first:
            scratch.insert(0, pltpu.VMEM((count, fetches * own_slots, order, order), p_values.dtype))
        product, window, *more = pl.pallas_call(
            functools.partial(
                multiply,
                kinds=tuple(kinds),
                chunk=chunk,
                ahead=ahead,
                block_rows=block_rows,
                kept=kept,
                news=tuple(news),
                first=first,
            ),
            out_shape=outs,
            in_specs=specs,
            out_specs=[ANY] + [VMEM] * (len(outs) - 1),
            scratch_shapes=scratch,
            input_output_aliases=aliases,
            compiler_params=pltpu.CompilerParams(vmem_limit_bytes=VMEM_GRANT),
        )(*inputs)
        ready = in_vmem(more[0]) if ahead else None
    return product


def solution(mesh):
    return jax.shard_map(
        steps,
        mesh=mesh,
        in_specs=(
            P("row", "col", None, None),
            P("row", "col"),
            P("row", "col", None, None),
            P("row", "col"),
            P("row", "col"),
        ),
        out_specs=P("row", "col", None, None),
        check_vma=False,
    )
```

```python
import functools

import jax
import jax.numpy as jnp
from jax import lax
from jax.experimental import pallas as pl
from jax.experimental.pallas import tpu as pltpu
from jax.sharding import PartitionSpec as P

VMEM_GRANT = 16 << 20
SECOND_EIGHTHS = (4, 4)
ANY = pl.BlockSpec(memory_space=pl.ANY)
SMEM = pl.BlockSpec(memory_space=pltpu.SMEM)
VMEM = pl.BlockSpec(memory_space=pltpu.VMEM)


def in_vmem(array):
    return pltpu.with_memory_space_constraint(array, pltpu.VMEM)


def in_hbm(array):
    return pltpu.with_memory_space_constraint(array, pltpu.HBM)


def row_chunks(block_rows):
    reach = block_rows // 2
    middle = reach // 2
    chunks = [(middle, reach), (0, middle)] if middle else [(0, reach)]
    start = reach
    for eighths in SECOND_EIGHTHS:
        stop = min(block_rows, start + max(1, eighths * reach // 8))
        if start < stop:
            chunks.append((start, stop))
            start = stop
    if start < block_rows:
        chunks.append((start, block_rows))
    return chunks


def halo_part(chunk, block_rows):
    start, stop = chunk
    reach = block_rows // 2
    if start < reach:
        return reach - stop, reach - start
    return block_rows + reach - stop, block_rows + reach - start


def local_start(part, block_rows, flip):
    start, stop = part
    return jnp.where(flip == 1, block_rows - stop, start)


def window_start(part, block_rows, flip):
    start, stop = part
    reach = block_rows // 2
    if start < reach:
        return jnp.where(flip == 1, reach + block_rows + start, reach - stop)
    return jnp.where(flip == 1, start - block_rows + reach, reach + 2 * block_rows - stop)


def cut(flips, p_values, s_values, cuts):
    block_rows = p_values.shape[0]
    sources = (p_values, s_values)

    def body(flips_ref, *refs):
        ins, outs, sems = refs[:2], refs[2:-1], refs[-1]
        copies = [
            pltpu.make_async_copy(
                ins[source].at[
                    pl.ds(local_start(part, block_rows, flips_ref[source]), out.shape[0])
                ],
                out,
                sems.at[n],
            )
            for n, ((source, part), out) in enumerate(zip(cuts, outs))
        ]
        for copy in copies:
            copy.start()
        for copy in copies:
            copy.wait()

    shapes = [
        jax.ShapeDtypeStruct((part[1] - part[0],) + sources[source].shape[1:], p_values.dtype)
        for source, part in cuts
    ]
    return list(
        pl.pallas_call(
            body,
            out_shape=shapes,
            in_specs=[SMEM, ANY, ANY],
            out_specs=[VMEM] * len(shapes),
            scratch_shapes=[pltpu.SemaphoreType.DMA((len(cuts),))],
            compiler_params=pltpu.CompilerParams(vmem_limit_bytes=VMEM_GRANT),
        )(flips, in_hbm(p_values), in_hbm(s_values))
    )


def find_places(first_ref, flip_ref, own_ref, near_ref, *refs, total_rows, both):
    far_ref = refs[0] if both else None
    kept_ref, *p_refs, place_ref = refs[1 if both else 0 :]
    kept, block_rows = kept_ref.shape
    s_slots, reach = own_ref.shape[0], block_rows // 2
    shape = place_ref.shape
    lane = lax.broadcasted_iota(jnp.int32, shape, 1)
    p_cols = jnp.full(shape, -1, jnp.int32)
    k = 0
    for ref in p_refs:
        cols = ref[...].T
        for slot in range(cols.shape[1]):
            p_cols = jnp.where(lane // kept == k, cols[:, slot : slot + 1], p_cols)
            k += 1
    wanted = jnp.full(shape, -2, jnp.int32)
    cols = kept_ref[...].T
    for m in range(kept):
        wanted = jnp.where(lane % kept == m, cols[:, m : m + 1], wanted)
    wanted = jnp.where(wanted < 0, -2, wanted)
    first_row = first_ref[0]
    local = p_cols - first_row
    local = jnp.where(local < 0, local + total_rows, local)
    local = jnp.where(local >= total_rows, local - total_rows, local)
    local = jnp.where(p_cols < 0, -1, local)
    flipped = flip_ref[0] == 1
    none = 2 * block_rows * s_slots
    place = jnp.full(shape, none, jnp.int32)
    for q in range(2 * block_rows):
        here = local == q
        for slot in range(s_slots):
            if reach <= q < reach + block_rows:
                col = own_ref[slot, q - reach]
            else:
                row = q + reach if q < reach else q - reach - block_rows
                far = far_ref[slot, row] if both else jnp.int32(-1)
                low_near = (q < reach) != flipped
                col = jnp.where(low_near, near_ref[slot, row], far)
            place = jnp.where(here & (wanted == col), q * s_slots + slot, place)
    place_ref[...] = place


def multiply(*refs, kinds, chunk, ahead, block_rows, kept, news, first):
    refs = list(refs)
    take = lambda count: [refs.pop(0) for _ in range(count)]
    flips_ref, place_ref = take(2)
    p_refs, new_refs = take(len(kinds)), take(len(news))
    take(0 if first else 2)
    ahead_refs = take(kinds.count("fetch") if ahead else 0)
    out_ref, window = take(2)
    next_ref = take(1)[0] if ahead else None
    lefts = take(1)[0] if first else None
    results, new_sem, p_sems, out_sems, next_sem = refs
    flip = flips_ref[0]
    start = local_start(chunk, block_rows, flip)
    count = chunk[1] - chunk[0]
    s_slots = (window.shape[0] - 1) // (2 * block_rows)
    own_slots = place_ref.shape[1] // (kept * len(kinds))
    wide = max(w for w in (4, 2, 1) if kept % w == 0)
    order = window.shape[1]
    slots = own_slots * len(kinds)
    fetched = [n for n, kind in enumerate(kinds) if kind == "fetch"]

    def fetch(i, n):
        return pltpu.make_async_copy(
            p_refs[n].at[i if n == 0 else start + i],
            lefts.at[i, pl.ds(fetched.index(n) * own_slots, own_slots)],
            p_sems.at[i],
        )

    def store(i, m):
        return pltpu.make_async_copy(
            results.at[i % 2, pl.ds(m, wide)],
            out_ref.at[start + i, pl.ds(m, wide)],
            out_sems.at[i % 2],
        )

    def stored(i):
        return pltpu.make_async_copy(
            results.at[i % 2], out_ref.at[start + i], out_sems.at[i % 2]
        )

    def left_blocks(i):
        for n, ref in enumerate(p_refs):
            for slot in range(own_slots):
                if kinds[n] != "fetch":
                    yield ref[i, slot]
                else:
                    source = lefts if first else p_refs[0]
                    yield source[i, fetched.index(n) * own_slots + slot]

    copies, moves = [], []
    for n, (ref, part) in enumerate(zip(new_refs, news)):
        at = block_rows // 2 if part is None else window_start(part, block_rows, flip)
        if first:
            target = window.at[pl.ds(at * s_slots, ref.shape[0] * s_slots)]
            target = target.reshape(ref.shape)
            copies.append(pltpu.make_async_copy(ref, target, new_sem.at[n]))
        else:
            moves.append((ref, at))
    for copy in copies:
        copy.start()
    if first:
        for i in range(count):
            for n in fetched:
                fetch(i, n).start()
        window[window.shape[0] - 1] = jnp.zeros(window.shape[1:], window.dtype)
    if ahead:
        next_start = local_start(ahead, block_rows, flip)
        next_count = ahead[1] - ahead[0]
        later = [
            pltpu.make_async_copy(
                ref.at[pl.ds(next_start if n else 0, next_count)],
                next_ref.at[:, pl.ds(n * own_slots, own_slots)],
                next_sem.at[n],
            )
            for n, ref in enumerate(ahead_refs)
        ]
        for copy in later:
            copy.start()
    for ref, at in moves:
        for row in range(ref.shape[0]):
            for slot in range(s_slots):
                window[(at + row) * s_slots + slot] = ref[row, slot]
    for copy in copies:
        copy.wait()

    def one_row(i, carry):
        if first:
            pltpu.make_async_copy(lefts.at[i], lefts.at[i], p_sems.at[i]).wait()

        @pl.when(i >= 2)
        def _():
            stored(i - 2).wait()

        left = jnp.concatenate(list(left_blocks(i)), axis=1)
        for m in range(0, kept, wide):
            right = jnp.concatenate(
                [
                    jnp.concatenate(
                        [
                            window[place_ref[start + i, k * kept + m + n]]
                            for n in range(wide)
                        ],
                        axis=1,
                    )
                    for k in range(slots)
                ],
                axis=0,
            )
            result = jnp.dot(left, right, preferred_element_type=jnp.float32)
            for n in range(wide):
                results[i % 2, m + n] = result[:, n * order : (n + 1) * order]
            store(i, m).start()
        return carry

    lax.fori_loop(0, count, one_row, 0)
    for i in range(max(0, count - 2), count):
        stored(i).wait()
    if ahead:
        for copy in later:
            copy.wait()


def turn_pairs(count, step):
    return [(i, (i + step) % count) for i in range(count)]


def far_pieces(own):
    count = lax.axis_size("col")
    held = [own]
    if count & (count - 1):
        for step in range(1, count):
            held.append(lax.ppermute(own, "col", turn_pairs(count, step)))
        return held
    step = count // 2
    while step > 1:
        swap = [(i, i ^ step) for i in range(count)]
        held = held + [lax.ppermute(piece, "col", swap) for piece in held]
        step //= 2
    return held


def passed_pieces(pieces):
    count = lax.axis_size("col")
    if count == 1 or count & (count - 1):
        return []
    return [
        lax.ppermute(piece, "col", [(i, i ^ 1) for i in range(count)]) for piece in pieces
    ]


def steps(p_values, p_cols, s_values, s_cols, c_cols):
    block_rows, own_slots, order, _ = p_values.shape
    s_slots, kept = s_values.shape[1], c_cols.shape[1]
    reach = block_rows // 2
    row_count = lax.axis_size("row")
    first_row = lax.axis_index("row") * block_rows - reach
    if row_count % 2 == 0:
        first_pairs = [(i, (i + (1 if i % 2 else -1)) % row_count) for i in range(row_count)]
        second_pairs = [(i, i ^ 1) for i in range(row_count)]
        odd = (lax.axis_index("row") % 2).astype(jnp.int32)
        flips = jnp.stack([odd, odd])
    else:
        first_pairs, second_pairs = turn_pairs(row_count, 1), turn_pairs(row_count, -1)
        flips = jnp.arange(2, dtype=jnp.int32)
    chunks = row_chunks(block_rows)
    sides = [halo_part(chunk, block_rows) for chunk in chunks]

    lead = next(n for n, chunk in enumerate(chunks) if chunk[0] >= reach)
    wanted = [(0, chunk) for chunk in chunks] + [(1, side) for side in sides]
    early = [0, len(chunks) + lead]
    late = [n for n in range(len(wanted)) if n not in early]
    pieces = dict(zip(early, cut(flips, p_values, s_values, [wanted[n] for n in early])))
    pieces |= zip(late, cut(flips, p_values, s_values, [wanted[n] for n in late]))
    own = [pieces[n] for n in range(len(chunks))]
    sent = [pieces[len(chunks) + n] for n in range(len(chunks))]

    far = [far_pieces(piece) for piece in own]
    halo = []
    for n, piece in enumerate(sent):
        pairs = first_pairs if chunks[n][0] < reach else second_pairs
        halo.append(lax.ppermute(piece, "row", pairs))
    core = passed_pieces([p_values])
    far_cols = far_pieces(p_cols.T)
    passed_cols = passed_pieces(far_cols)
    first_cols = lax.ppermute(s_cols.T, "row", first_pairs)
    second_cols = lax.ppermute(s_cols.T, "row", second_pairs)

    col_pieces = far_cols + passed_cols

    def places(both):
        tables = [first_row[None], flips, s_cols.T, first_cols] + ([second_cols] if both else [])
        return pl.pallas_call(
            functools.partial(find_places, total_rows=block_rows * row_count, both=both),
            out_shape=jax.ShapeDtypeStruct(
                (block_rows, len(col_pieces) * own_slots * kept), jnp.int32
            ),
            in_specs=[SMEM] * len(tables) + [VMEM] * (1 + len(col_pieces)),
            out_specs=VMEM,
            compiler_params=pltpu.CompilerParams(vmem_limit_bytes=VMEM_GRANT),
        )(*tables, c_cols.T, *col_pieces)

    place_of = [places(False), places(True)]

    product = window = ready = None
    window_shape = (2 * block_rows * s_slots + 1, order, order)
    fetches = 1 + len(core)
    for n, chunk in enumerate(chunks):
        first = product is None
        count = chunk[1] - chunk[0]
        ahead = chunks[n + 1] if n + 1 < len(chunks) else None
        passed = passed_pieces(far[n][1:])
        kinds = ["fetch"] + ["here"] * len(far[n][1:]) + ["fetch"] * len(core)
        kinds += ["here"] * len(passed)
        fetch_from = [far[n][0]] + core
        here = far[n][1:] + passed
        inputs, specs = [flips, place_of[chunk[0] >= reach]], [SMEM] * 2
        for kind in kinds:
            if kind == "here":
                keep_in = in_vmem if ahead is None or len(here) <= len(passed) else lambda x: x
                inputs.append(keep_in(here.pop(0)))
            else:
                inputs.append(in_hbm(fetch_from.pop(0)) if first else ready)
            specs.append(ANY if first and kind == "fetch" else VMEM)
        aliases = {}
        if first:
            news = [None, sides[n]]
            inputs += [in_hbm(s_values), in_hbm(halo[n])]
            specs += [ANY] * 2
        else:
            news = [sides[n]]
            inputs.append(halo[n] if ahead else in_vmem(halo[n]))
            specs.append(VMEM)
            aliases = {len(inputs): 1, len(inputs) + 1: 0}
            inputs += [in_vmem(window), product]
            specs += [VMEM, ANY]
        outs = [
            jax.ShapeDtypeStruct((block_rows, kept, order, order), jnp.float32),
            pltpu.VMEM(window_shape, s_values.dtype),
        ]
        if ahead:
            inputs += [in_hbm(own[n + 1])] + [in_hbm(piece) for piece in core]
            specs += [ANY] * fetches
            shape = (ahead[1] - ahead[0], fetches * own_slots, order, order)
            outs.append(pltpu.VMEM(shape, p_values.dtype))
        scratch = [
            pltpu.VMEM((2, kept, order, order), jnp.float32),
            pltpu.SemaphoreType.DMA((2,)),
            pltpu.SemaphoreType.DMA((count,)),
            pltpu.SemaphoreType.DMA((2,)),
            pltpu.SemaphoreType.DMA((fetches,)),
        ]
        if first:
            scratch.insert(0, pltpu.VMEM((count, fetches * own_slots, order, order), p_values.dtype))
        product, window, *more = pl.pallas_call(
            functools.partial(
                multiply,
                kinds=tuple(kinds),
                chunk=chunk,
                ahead=ahead,
                block_rows=block_rows,
                kept=kept,
                news=tuple(news),
                first=first,
            ),
            out_shape=outs,
            in_specs=specs,
            out_specs=[ANY] + [VMEM] * (len(outs) - 1),
            scratch_shapes=scratch,
            input_output_aliases=aliases,
            compiler_params=pltpu.CompilerParams(vmem_limit_bytes=VMEM_GRANT),
        )(*inputs)
        ready = in_vmem(more[0]) if ahead else None
    return product


def solution(mesh):
    return jax.shard_map(
        steps,
        mesh=mesh,
        in_specs=(
            P("row", "col", None, None),
            P("row", "col"),
            P("row", "col", None, None),
            P("row", "col"),
            P("row", "col"),
        ),
        out_specs=P("row", "col", None, None),
        check_vma=False,
    )
```

```python
import functools

import jax
import jax.numpy as jnp
from jax import lax
from jax.experimental import pallas as pl
from jax.experimental.pallas import tpu as pltpu
from jax.sharding import PartitionSpec as P

VMEM_GRANT = 16 << 20
SECOND_EIGHTHS = (4, 4)
ANY = pl.BlockSpec(memory_space=pl.ANY)
SMEM = pl.BlockSpec(memory_space=pltpu.SMEM)
VMEM = pl.BlockSpec(memory_space=pltpu.VMEM)


def in_vmem(array):
    return pltpu.with_memory_space_constraint(array, pltpu.VMEM)


def in_hbm(array):
    return pltpu.with_memory_space_constraint(array, pltpu.HBM)


def row_chunks(block_rows):
    reach = block_rows // 2
    middle = reach // 2
    chunks = [(middle, reach), (0, middle)] if middle else [(0, reach)]
    start = reach
    for eighths in SECOND_EIGHTHS:
        stop = min(block_rows, start + max(1, eighths * reach // 8))
        if start < stop:
            chunks.append((start, stop))
            start = stop
    if start < block_rows:
        chunks.append((start, block_rows))
    return chunks


def halo_part(chunk, block_rows):
    start, stop = chunk
    reach = block_rows // 2
    if start < reach:
        return reach - stop, reach - start
    return block_rows + reach - stop, block_rows + reach - start


def local_start(part, block_rows, flip):
    start, stop = part
    return jnp.where(flip == 1, block_rows - stop, start)


def window_start(part, block_rows, flip):
    start, stop = part
    reach = block_rows // 2
    if start < reach:
        return jnp.where(flip == 1, reach + block_rows + start, reach - stop)
    return jnp.where(flip == 1, start - block_rows + reach, reach + 2 * block_rows - stop)


def cut(p_values, s_values, cuts):
    block_rows = p_values.shape[0]
    sources = (p_values, s_values)

    even = lax.axis_size("row") % 2 == 0

    def body(*refs):
        ins, outs, sems = refs[:2], refs[2:-1], refs[-1]
        odd = lax.axis_index("row") % 2
        copies = [
            pltpu.make_async_copy(
                ins[source].at[
                    pl.ds(local_start(part, block_rows, odd if even else source), out.shape[0])
                ],
                out,
                sems.at[n],
            )
            for n, ((source, part), out) in enumerate(zip(cuts, outs))
        ]
        for copy in copies:
            copy.start()
        for copy in copies:
            copy.wait()

    shapes = [
        jax.ShapeDtypeStruct((part[1] - part[0],) + sources[source].shape[1:], p_values.dtype)
        for source, part in cuts
    ]
    return list(
        pl.pallas_call(
            body,
            out_shape=shapes,
            in_specs=[ANY, ANY],
            out_specs=[VMEM] * len(shapes),
            scratch_shapes=[pltpu.SemaphoreType.DMA((len(cuts),))],
            compiler_params=pltpu.CompilerParams(vmem_limit_bytes=VMEM_GRANT),
        )(in_hbm(p_values), in_hbm(s_values))
    )


def find_places(first_ref, flip_ref, own_ref, near_ref, *refs, total_rows, both):
    far_ref = refs[0] if both else None
    kept_ref, *p_refs, place_ref = refs[1 if both else 0 :]
    kept, block_rows = kept_ref.shape
    s_slots, reach = own_ref.shape[0], block_rows // 2
    shape = place_ref.shape
    lane = lax.broadcasted_iota(jnp.int32, shape, 1)
    p_cols = jnp.full(shape, -1, jnp.int32)
    k = 0
    for ref in p_refs:
        cols = ref[...].T
        for slot in range(cols.shape[1]):
            p_cols = jnp.where(lane // kept == k, cols[:, slot : slot + 1], p_cols)
            k += 1
    wanted = jnp.full(shape, -2, jnp.int32)
    cols = kept_ref[...].T
    for m in range(kept):
        wanted = jnp.where(lane % kept == m, cols[:, m : m + 1], wanted)
    wanted = jnp.where(wanted < 0, -2, wanted)
    first_row = first_ref[0]
    local = p_cols - first_row
    local = jnp.where(local < 0, local + total_rows, local)
    local = jnp.where(local >= total_rows, local - total_rows, local)
    local = jnp.where(p_cols < 0, -1, local)
    flipped = flip_ref[0] == 1
    none = 2 * block_rows * s_slots
    place = jnp.full(shape, none, jnp.int32)
    for q in range(2 * block_rows):
        here = local == q
        for slot in range(s_slots):
            if reach <= q < reach + block_rows:
                col = own_ref[slot, q - reach]
            else:
                row = q + reach if q < reach else q - reach - block_rows
                far = far_ref[slot, row] if both else jnp.int32(-1)
                low_near = (q < reach) != flipped
                col = jnp.where(low_near, near_ref[slot, row], far)
            place = jnp.where(here & (wanted == col), q * s_slots + slot, place)
    place_ref[...] = place


def multiply(*refs, kinds, chunk, ahead, block_rows, kept, news, first):
    refs = list(refs)
    take = lambda count: [refs.pop(0) for _ in range(count)]
    flips_ref, place_ref = take(2)
    p_refs, new_refs = take(len(kinds)), take(len(news))
    take(0 if first else 2)
    ahead_refs = take(kinds.count("fetch") if ahead else 0)
    out_ref, window = take(2)
    next_ref = take(1)[0] if ahead else None
    lefts = take(1)[0] if first else None
    results, new_sem, p_sems, out_sems, next_sem = refs
    flip = flips_ref[0]
    start = local_start(chunk, block_rows, flip)
    count = chunk[1] - chunk[0]
    s_slots = (window.shape[0] - 1) // (2 * block_rows)
    own_slots = place_ref.shape[1] // (kept * len(kinds))
    wide = max(w for w in (4, 2, 1) if kept % w == 0)
    order = window.shape[1]
    slots = own_slots * len(kinds)
    fetched = [n for n, kind in enumerate(kinds) if kind == "fetch"]

    def fetch(i, n):
        return pltpu.make_async_copy(
            p_refs[n].at[i if n == 0 else start + i],
            lefts.at[i, pl.ds(fetched.index(n) * own_slots, own_slots)],
            p_sems.at[i],
        )

    def store(i, m):
        return pltpu.make_async_copy(
            results.at[i % 2, pl.ds(m, wide)],
            out_ref.at[start + i, pl.ds(m, wide)],
            out_sems.at[i % 2],
        )

    def stored(i):
        return pltpu.make_async_copy(
            results.at[i % 2], out_ref.at[start + i], out_sems.at[i % 2]
        )

    def left_blocks(i):
        for n, ref in enumerate(p_refs):
            for slot in range(own_slots):
                if kinds[n] != "fetch":
                    yield ref[i, slot]
                else:
                    source = lefts if first else p_refs[0]
                    yield source[i, fetched.index(n) * own_slots + slot]

    copies, moves = [], []
    for n, (ref, part) in enumerate(zip(new_refs, news)):
        at = block_rows // 2 if part is None else window_start(part, block_rows, flip)
        if first:
            target = window.at[pl.ds(at * s_slots, ref.shape[0] * s_slots)]
            target = target.reshape(ref.shape)
            copies.append(pltpu.make_async_copy(ref, target, new_sem.at[n]))
        else:
            moves.append((ref, at))
    for copy in copies:
        copy.start()
    if first:
        for i in range(count):
            for n in fetched:
                fetch(i, n).start()
        window[window.shape[0] - 1] = jnp.zeros(window.shape[1:], window.dtype)
    if ahead:
        next_start = local_start(ahead, block_rows, flip)
        next_count = ahead[1] - ahead[0]
        later = [
            pltpu.make_async_copy(
                ref.at[pl.ds(next_start if n else 0, next_count)],
                next_ref.at[:, pl.ds(n * own_slots, own_slots)],
                next_sem.at[n],
            )
            for n, ref in enumerate(ahead_refs)
        ]
        for copy in later:
            copy.start()
    for ref, at in moves:
        for row in range(ref.shape[0]):
            for slot in range(s_slots):
                window[(at + row) * s_slots + slot] = ref[row, slot]
    for copy in copies:
        copy.wait()

    def one_row(i, carry):
        if first:
            pltpu.make_async_copy(lefts.at[i], lefts.at[i], p_sems.at[i]).wait()

        @pl.when(i >= 2)
        def _():
            stored(i - 2).wait()

        left = jnp.concatenate(list(left_blocks(i)), axis=1)
        for m in range(0, kept, wide):
            right = jnp.concatenate(
                [
                    jnp.concatenate(
                        [
                            window[place_ref[start + i, k * kept + m + n]]
                            for n in range(wide)
                        ],
                        axis=1,
                    )
                    for k in range(slots)
                ],
                axis=0,
            )
            result = jnp.dot(left, right, preferred_element_type=jnp.float32)
            for n in range(wide):
                results[i % 2, m + n] = result[:, n * order : (n + 1) * order]
            store(i, m).start()
        return carry

    lax.fori_loop(0, count, one_row, 0)
    for i in range(max(0, count - 2), count):
        stored(i).wait()
    if ahead:
        for copy in later:
            copy.wait()


def turn_pairs(count, step):
    return [(i, (i + step) % count) for i in range(count)]


def far_pieces(own):
    count = lax.axis_size("col")
    held = [own]
    if count & (count - 1):
        for step in range(1, count):
            held.append(lax.ppermute(own, "col", turn_pairs(count, step)))
        return held
    step = count // 2
    while step > 1:
        swap = [(i, i ^ step) for i in range(count)]
        held = held + [lax.ppermute(piece, "col", swap) for piece in held]
        step //= 2
    return held


def passed_pieces(pieces):
    count = lax.axis_size("col")
    if count == 1 or count & (count - 1):
        return []
    return [
        lax.ppermute(piece, "col", [(i, i ^ 1) for i in range(count)]) for piece in pieces
    ]


def steps(p_values, p_cols, s_values, s_cols, c_cols):
    block_rows, own_slots, order, _ = p_values.shape
    s_slots, kept = s_values.shape[1], c_cols.shape[1]
    reach = block_rows // 2
    row_count = lax.axis_size("row")
    first_row = lax.axis_index("row") * block_rows - reach
    if row_count % 2 == 0:
        first_pairs = [(i, (i + (1 if i % 2 else -1)) % row_count) for i in range(row_count)]
        second_pairs = [(i, i ^ 1) for i in range(row_count)]
        odd = (lax.axis_index("row") % 2).astype(jnp.int32)
        flips = jnp.stack([odd, odd])
    else:
        first_pairs, second_pairs = turn_pairs(row_count, 1), turn_pairs(row_count, -1)
        flips = jnp.arange(2, dtype=jnp.int32)
    chunks = row_chunks(block_rows)
    sides = [halo_part(chunk, block_rows) for chunk in chunks]

    lead = next(n for n, chunk in enumerate(chunks) if chunk[0] >= reach)
    wanted = [(0, chunk) for chunk in chunks] + [(1, side) for side in sides]
    early = [0, len(chunks) + lead]
    late = [n for n in range(len(wanted)) if n not in early]
    pieces = dict(zip(early, cut(p_values, s_values, [wanted[n] for n in early])))
    pieces |= zip(late, cut(p_values, s_values, [wanted[n] for n in late]))
    own = [pieces[n] for n in range(len(chunks))]
    sent = [pieces[len(chunks) + n] for n in range(len(chunks))]

    far = [far_pieces(piece) for piece in own]
    halo = []
    for n, piece in enumerate(sent):
        pairs = first_pairs if chunks[n][0] < reach else second_pairs
        halo.append(lax.ppermute(piece, "row", pairs))
    core = passed_pieces([p_values])
    far_cols = far_pieces(p_cols.T)
    passed_cols = passed_pieces(far_cols)
    first_cols = lax.ppermute(s_cols.T, "row", first_pairs)
    second_cols = lax.ppermute(s_cols.T, "row", second_pairs)

    col_pieces = far_cols + passed_cols

    def places(both):
        tables = [first_row[None], flips, s_cols.T, first_cols] + ([second_cols] if both else [])
        return pl.pallas_call(
            functools.partial(find_places, total_rows=block_rows * row_count, both=both),
            out_shape=jax.ShapeDtypeStruct(
                (block_rows, len(col_pieces) * own_slots * kept), jnp.int32
            ),
            in_specs=[SMEM] * len(tables) + [VMEM] * (1 + len(col_pieces)),
            out_specs=VMEM,
            compiler_params=pltpu.CompilerParams(vmem_limit_bytes=VMEM_GRANT),
        )(*tables, c_cols.T, *col_pieces)

    place_of = [places(False), places(True)]

    product = window = ready = None
    window_shape = (2 * block_rows * s_slots + 1, order, order)
    fetches = 1 + len(core)
    for n, chunk in enumerate(chunks):
        first = product is None
        count = chunk[1] - chunk[0]
        ahead = chunks[n + 1] if n + 1 < len(chunks) else None
        passed = passed_pieces(far[n][1:])
        kinds = ["fetch"] + ["here"] * len(far[n][1:]) + ["fetch"] * len(core)
        kinds += ["here"] * len(passed)
        fetch_from = [far[n][0]] + core
        here = far[n][1:] + passed
        inputs, specs = [flips, place_of[chunk[0] >= reach]], [SMEM] * 2
        for kind in kinds:
            if kind == "here":
                keep_in = in_vmem if ahead is None or len(here) <= len(passed) else lambda x: x
                inputs.append(keep_in(here.pop(0)))
            else:
                inputs.append(in_hbm(fetch_from.pop(0)) if first else ready)
            specs.append(ANY if first and kind == "fetch" else VMEM)
        aliases = {}
        if first:
            news = [None, sides[n]]
            inputs += [in_hbm(s_values), in_hbm(halo[n])]
            specs += [ANY] * 2
        else:
            news = [sides[n]]
            inputs.append(halo[n] if ahead else in_vmem(halo[n]))
            specs.append(VMEM)
            aliases = {len(inputs): 1, len(inputs) + 1: 0}
            inputs += [in_vmem(window), product]
            specs += [VMEM, ANY]
        outs = [
            jax.ShapeDtypeStruct((block_rows, kept, order, order), jnp.float32),
            pltpu.VMEM(window_shape, s_values.dtype),
        ]
        if ahead:
            inputs += [in_hbm(own[n + 1])] + [in_hbm(piece) for piece in core]
            specs += [ANY] * fetches
            shape = (ahead[1] - ahead[0], fetches * own_slots, order, order)
            outs.append(pltpu.VMEM(shape, p_values.dtype))
        scratch = [
            pltpu.VMEM((2, kept, order, order), jnp.float32),
            pltpu.SemaphoreType.DMA((2,)),
            pltpu.SemaphoreType.DMA((count,)),
            pltpu.SemaphoreType.DMA((2,)),
            pltpu.SemaphoreType.DMA((fetches,)),
        ]
        if first:
            scratch.insert(0, pltpu.VMEM((count, fetches * own_slots, order, order), p_values.dtype))
        product, window, *more = pl.pallas_call(
            functools.partial(
                multiply,
                kinds=tuple(kinds),
                chunk=chunk,
                ahead=ahead,
                block_rows=block_rows,
                kept=kept,
                news=tuple(news),
                first=first,
            ),
            out_shape=outs,
            in_specs=specs,
            out_specs=[ANY] + [VMEM] * (len(outs) - 1),
            scratch_shapes=scratch,
            input_output_aliases=aliases,
            compiler_params=pltpu.CompilerParams(vmem_limit_bytes=VMEM_GRANT),
        )(*inputs)
        ready = in_vmem(more[0]) if ahead else None
    return product


def solution(mesh):
    return jax.shard_map(
        steps,
        mesh=mesh,
        in_specs=(
            P("row", "col", None, None),
            P("row", "col"),
            P("row", "col", None, None),
            P("row", "col"),
            P("row", "col"),
        ),
        out_specs=P("row", "col", None, None),
        check_vma=False,
    )
```

```python
import functools

import jax
import jax.numpy as jnp
from jax import lax
from jax.experimental import pallas as pl
from jax.experimental.pallas import tpu as pltpu
from jax.sharding import PartitionSpec as P

VMEM_GRANT = 16 << 20
SECOND_EIGHTHS = (4, 4)
ANY = pl.BlockSpec(memory_space=pl.ANY)
SMEM = pl.BlockSpec(memory_space=pltpu.SMEM)
VMEM = pl.BlockSpec(memory_space=pltpu.VMEM)


def in_vmem(array):
    return pltpu.with_memory_space_constraint(array, pltpu.VMEM)


def in_hbm(array):
    return pltpu.with_memory_space_constraint(array, pltpu.HBM)


def row_chunks(block_rows):
    reach = block_rows // 2
    middle = reach // 2
    chunks = [(middle, reach), (0, middle)] if middle else [(0, reach)]
    start = reach
    for eighths in SECOND_EIGHTHS:
        stop = min(block_rows, start + max(1, eighths * reach // 8))
        if start < stop:
            chunks.append((start, stop))
            start = stop
    if start < block_rows:
        chunks.append((start, block_rows))
    return chunks


def halo_part(chunk, block_rows):
    start, stop = chunk
    reach = block_rows // 2
    if start < reach:
        return reach - stop, reach - start
    return block_rows + reach - stop, block_rows + reach - start


def local_start(part, block_rows, flip):
    start, stop = part
    return jnp.where(flip == 1, block_rows - stop, start)


def window_start(part, block_rows, flip):
    start, stop = part
    reach = block_rows // 2
    if start < reach:
        return jnp.where(flip == 1, reach + block_rows + start, reach - stop)
    return jnp.where(flip == 1, start - block_rows + reach, reach + 2 * block_rows - stop)


def cut(p_values, s_values, cuts):
    block_rows = p_values.shape[0]
    sources = (p_values, s_values)

    even = lax.axis_size("row") % 2 == 0

    def body(*refs):
        ins, outs, sems = refs[:2], refs[2:-1], refs[-1]
        odd = lax.axis_index("row") % 2
        copies = [
            pltpu.make_async_copy(
                ins[source].at[
                    pl.ds(local_start(part, block_rows, odd if even else source), out.shape[0])
                ],
                out,
                sems.at[n],
            )
            for n, ((source, part), out) in enumerate(zip(cuts, outs))
        ]
        for copy in copies:
            copy.start()
        for copy in copies:
            copy.wait()

    shapes = [
        jax.ShapeDtypeStruct((part[1] - part[0],) + sources[source].shape[1:], p_values.dtype)
        for source, part in cuts
    ]
    return list(
        pl.pallas_call(
            body,
            out_shape=shapes,
            in_specs=[ANY, ANY],
            out_specs=[VMEM] * len(shapes),
            scratch_shapes=[pltpu.SemaphoreType.DMA((len(cuts),))],
            compiler_params=pltpu.CompilerParams(vmem_limit_bytes=VMEM_GRANT),
        )(in_hbm(p_values), in_hbm(s_values))
    )


def find_places(first_ref, flip_ref, own_ref, near_ref, *refs, total_rows, both):
    far_ref = refs[0] if both else None
    kept_ref, *p_refs, place_ref = refs[1 if both else 0 :]
    kept, block_rows = kept_ref.shape
    s_slots, reach = own_ref.shape[0], block_rows // 2
    shape = place_ref.shape
    lane = lax.broadcasted_iota(jnp.int32, shape, 1)
    p_cols = jnp.full(shape, -1, jnp.int32)
    k = 0
    for ref in p_refs:
        cols = ref[...].T
        for slot in range(cols.shape[1]):
            p_cols = jnp.where(lane // kept == k, cols[:, slot : slot + 1], p_cols)
            k += 1
    wanted = jnp.full(shape, -2, jnp.int32)
    cols = kept_ref[...].T
    for m in range(kept):
        wanted = jnp.where(lane % kept == m, cols[:, m : m + 1], wanted)
    wanted = jnp.where(wanted < 0, -2, wanted)
    first_row = first_ref[0]
    local = p_cols - first_row
    local = jnp.where(local < 0, local + total_rows, local)
    local = jnp.where(local >= total_rows, local - total_rows, local)
    local = jnp.where(p_cols < 0, -1, local)
    flipped = flip_ref[0] == 1
    none = 2 * block_rows * s_slots
    place = jnp.full(shape, none, jnp.int32)
    for q in range(2 * block_rows):
        here = local == q
        for slot in range(s_slots):
            if reach <= q < reach + block_rows:
                col = own_ref[slot, q - reach]
            else:
                row = q + reach if q < reach else q - reach - block_rows
                far = far_ref[slot, row] if both else jnp.int32(-1)
                low_near = (q < reach) != flipped
                col = jnp.where(low_near, near_ref[slot, row], far)
            place = jnp.where(here & (wanted == col), q * s_slots + slot, place)
    place_ref[...] = place


def multiply(*refs, kinds, chunk, ahead, block_rows, kept, news, first):
    refs = list(refs)
    take = lambda count: [refs.pop(0) for _ in range(count)]
    (place_ref,) = take(1)
    p_refs, new_refs = take(len(kinds)), take(len(news))
    take(0 if first else 2)
    ahead_refs = take(kinds.count("fetch") if ahead else 0)
    out_ref, window = take(2)
    next_ref = take(1)[0] if ahead else None
    lefts = take(1)[0] if first else None
    results, new_sem, p_sems, out_sems, next_sem = refs
    flip = lax.axis_index("row") % 2 if lax.axis_size("row") % 2 == 0 else 0
    start = local_start(chunk, block_rows, flip)
    count = chunk[1] - chunk[0]
    s_slots = (window.shape[0] - 1) // (2 * block_rows)
    own_slots = place_ref.shape[1] // (kept * len(kinds))
    wide = max(w for w in (4, 2, 1) if kept % w == 0)
    order = window.shape[1]
    slots = own_slots * len(kinds)
    fetched = [n for n, kind in enumerate(kinds) if kind == "fetch"]

    def fetch(i, n):
        return pltpu.make_async_copy(
            p_refs[n].at[i if n == 0 else start + i],
            lefts.at[i, pl.ds(fetched.index(n) * own_slots, own_slots)],
            p_sems.at[i],
        )

    def store(i, m):
        return pltpu.make_async_copy(
            results.at[i % 2, pl.ds(m, wide)],
            out_ref.at[start + i, pl.ds(m, wide)],
            out_sems.at[i % 2],
        )

    def stored(i):
        return pltpu.make_async_copy(
            results.at[i % 2], out_ref.at[start + i], out_sems.at[i % 2]
        )

    def left_blocks(i):
        for n, ref in enumerate(p_refs):
            for slot in range(own_slots):
                if kinds[n] != "fetch":
                    yield ref[i, slot]
                else:
                    source = lefts if first else p_refs[0]
                    yield source[i, fetched.index(n) * own_slots + slot]

    copies, moves = [], []
    for n, (ref, part) in enumerate(zip(new_refs, news)):
        at = block_rows // 2 if part is None else window_start(part, block_rows, flip)
        if first:
            target = window.at[pl.ds(at * s_slots, ref.shape[0] * s_slots)]
            target = target.reshape(ref.shape)
            copies.append(pltpu.make_async_copy(ref, target, new_sem.at[n]))
        else:
            moves.append((ref, at))
    for copy in copies:
        copy.start()
    if first:
        for i in range(count):
            for n in fetched:
                fetch(i, n).start()
        window[window.shape[0] - 1] = jnp.zeros(window.shape[1:], window.dtype)
    if ahead:
        next_start = local_start(ahead, block_rows, flip)
        next_count = ahead[1] - ahead[0]
        later = [
            pltpu.make_async_copy(
                ref.at[pl.ds(next_start if n else 0, next_count)],
                next_ref.at[:, pl.ds(n * own_slots, own_slots)],
                next_sem.at[n],
            )
            for n, ref in enumerate(ahead_refs)
        ]
        for copy in later:
            copy.start()
    for ref, at in moves:
        for row in range(ref.shape[0]):
            for slot in range(s_slots):
                window[(at + row) * s_slots + slot] = ref[row, slot]
    for copy in copies:
        copy.wait()

    def one_row(i, carry):
        if first:
            pltpu.make_async_copy(lefts.at[i], lefts.at[i], p_sems.at[i]).wait()

        @pl.when(i >= 2)
        def _():
            stored(i - 2).wait()

        left = jnp.concatenate(list(left_blocks(i)), axis=1)
        for m in range(0, kept, wide):
            right = jnp.concatenate(
                [
                    jnp.concatenate(
                        [
                            window[place_ref[start + i, k * kept + m + n]]
                            for n in range(wide)
                        ],
                        axis=1,
                    )
                    for k in range(slots)
                ],
                axis=0,
            )
            result = jnp.dot(left, right, preferred_element_type=jnp.float32)
            for n in range(wide):
                results[i % 2, m + n] = result[:, n * order : (n + 1) * order]
            store(i, m).start()
        return carry

    lax.fori_loop(0, count, one_row, 0)
    for i in range(max(0, count - 2), count):
        stored(i).wait()
    if ahead:
        for copy in later:
            copy.wait()


def turn_pairs(count, step):
    return [(i, (i + step) % count) for i in range(count)]


def far_pieces(own):
    count = lax.axis_size("col")
    held = [own]
    if count & (count - 1):
        for step in range(1, count):
            held.append(lax.ppermute(own, "col", turn_pairs(count, step)))
        return held
    step = count // 2
    while step > 1:
        swap = [(i, i ^ step) for i in range(count)]
        held = held + [lax.ppermute(piece, "col", swap) for piece in held]
        step //= 2
    return held


def passed_pieces(pieces):
    count = lax.axis_size("col")
    if count == 1 or count & (count - 1):
        return []
    return [
        lax.ppermute(piece, "col", [(i, i ^ 1) for i in range(count)]) for piece in pieces
    ]


def steps(p_values, p_cols, s_values, s_cols, c_cols):
    block_rows, own_slots, order, _ = p_values.shape
    s_slots, kept = s_values.shape[1], c_cols.shape[1]
    reach = block_rows // 2
    row_count = lax.axis_size("row")
    first_row = lax.axis_index("row") * block_rows - reach
    if row_count % 2 == 0:
        first_pairs = [(i, (i + (1 if i % 2 else -1)) % row_count) for i in range(row_count)]
        second_pairs = [(i, i ^ 1) for i in range(row_count)]
        odd = (lax.axis_index("row") % 2).astype(jnp.int32)
        flips = jnp.stack([odd, odd])
    else:
        first_pairs, second_pairs = turn_pairs(row_count, 1), turn_pairs(row_count, -1)
        flips = jnp.arange(2, dtype=jnp.int32)
    chunks = row_chunks(block_rows)
    sides = [halo_part(chunk, block_rows) for chunk in chunks]

    lead = next(n for n, chunk in enumerate(chunks) if chunk[0] >= reach)
    wanted = [(0, chunk) for chunk in chunks] + [(1, side) for side in sides]
    early = [0, len(chunks) + lead]
    late = [n for n in range(len(wanted)) if n not in early]
    pieces = dict(zip(early, cut(p_values, s_values, [wanted[n] for n in early])))
    pieces |= zip(late, cut(p_values, s_values, [wanted[n] for n in late]))
    own = [pieces[n] for n in range(len(chunks))]
    sent = [pieces[len(chunks) + n] for n in range(len(chunks))]

    far = [far_pieces(piece) for piece in own]
    halo = []
    for n, piece in enumerate(sent):
        pairs = first_pairs if chunks[n][0] < reach else second_pairs
        halo.append(lax.ppermute(piece, "row", pairs))
    core = passed_pieces([p_values])
    far_cols = far_pieces(p_cols.T)
    passed_cols = passed_pieces(far_cols)
    first_cols = lax.ppermute(s_cols.T, "row", first_pairs)
    second_cols = lax.ppermute(s_cols.T, "row", second_pairs)

    col_pieces = far_cols + passed_cols

    def places(both):
        tables = [first_row[None], flips, s_cols.T, first_cols] + ([second_cols] if both else [])
        return pl.pallas_call(
            functools.partial(find_places, total_rows=block_rows * row_count, both=both),
            out_shape=jax.ShapeDtypeStruct(
                (block_rows, len(col_pieces) * own_slots * kept), jnp.int32
            ),
            in_specs=[SMEM] * len(tables) + [VMEM] * (1 + len(col_pieces)),
            out_specs=VMEM,
            compiler_params=pltpu.CompilerParams(vmem_limit_bytes=VMEM_GRANT),
        )(*tables, c_cols.T, *col_pieces)

    place_of = [places(False), places(True)]

    product = window = ready = None
    window_shape = (2 * block_rows * s_slots + 1, order, order)
    fetches = 1 + len(core)
    for n, chunk in enumerate(chunks):
        first = product is None
        count = chunk[1] - chunk[0]
        ahead = chunks[n + 1] if n + 1 < len(chunks) else None
        passed = passed_pieces(far[n][1:])
        kinds = ["fetch"] + ["here"] * len(far[n][1:]) + ["fetch"] * len(core)
        kinds += ["here"] * len(passed)
        fetch_from = [far[n][0]] + core
        here = far[n][1:] + passed
        inputs, specs = [place_of[chunk[0] >= reach]], [SMEM]
        for kind in kinds:
            if kind == "here":
                keep_in = in_vmem if ahead is None or len(here) <= len(passed) else lambda x: x
                inputs.append(keep_in(here.pop(0)))
            else:
                inputs.append(in_hbm(fetch_from.pop(0)) if first else ready)
            specs.append(ANY if first and kind == "fetch" else VMEM)
        aliases = {}
        if first:
            news = [None, sides[n]]
            inputs += [in_hbm(s_values), in_hbm(halo[n])]
            specs += [ANY] * 2
        else:
            news = [sides[n]]
            inputs.append(halo[n] if ahead else in_vmem(halo[n]))
            specs.append(VMEM)
            aliases = {len(inputs): 1, len(inputs) + 1: 0}
            inputs += [in_vmem(window), product]
            specs += [VMEM, ANY]
        outs = [
            jax.ShapeDtypeStruct((block_rows, kept, order, order), jnp.float32),
            pltpu.VMEM(window_shape, s_values.dtype),
        ]
        if ahead:
            inputs += [in_hbm(own[n + 1])] + [in_hbm(piece) for piece in core]
            specs += [ANY] * fetches
            shape = (ahead[1] - ahead[0], fetches * own_slots, order, order)
            outs.append(pltpu.VMEM(shape, p_values.dtype))
        scratch = [
            pltpu.VMEM((2, kept, order, order), jnp.float32),
            pltpu.SemaphoreType.DMA((2,)),
            pltpu.SemaphoreType.DMA((count,)),
            pltpu.SemaphoreType.DMA((2,)),
            pltpu.SemaphoreType.DMA((fetches,)),
        ]
        if first:
            scratch.insert(0, pltpu.VMEM((count, fetches * own_slots, order, order), p_values.dtype))
        product, window, *more = pl.pallas_call(
            functools.partial(
                multiply,
                kinds=tuple(kinds),
                chunk=chunk,
                ahead=ahead,
                block_rows=block_rows,
                kept=kept,
                news=tuple(news),
                first=first,
            ),
            out_shape=outs,
            in_specs=specs,
            out_specs=[ANY] + [VMEM] * (len(outs) - 1),
            scratch_shapes=scratch,
            input_output_aliases=aliases,
            compiler_params=pltpu.CompilerParams(vmem_limit_bytes=VMEM_GRANT),
        )(*inputs)
        ready = in_vmem(more[0]) if ahead else None
    return product


def solution(mesh):
    return jax.shard_map(
        steps,
        mesh=mesh,
        in_specs=(
            P("row", "col", None, None),
            P("row", "col"),
            P("row", "col", None, None),
            P("row", "col"),
            P("row", "col"),
        ),
        out_specs=P("row", "col", None, None),
        check_vma=False,
    )
```
